32 devices in a mesh: fsdp: 16 (over z, y, core), expert: 2 (over x).
Axes of the slice: x: 2, y: 2, z: 4, core: 2. Of those that a mesh axis runs over, the one named last changes fastest.
Arguments:
- tokens: bfloat16 [8192, 1024], P(('fsdp', 'expert')), may hold values from -6 to 6
- query_weight: bfloat16 [1024, 1024], P(('fsdp', 'expert')), may hold values from -0.1875 to 0.1875
- key_projection: bfloat16 [1024, 512], P(('fsdp', 'expert')), may hold values from -0.1875 to 0.1875
- value_projection: bfloat16 [1024, 512], P(('fsdp', 'expert')), may hold values from -0.1875 to 0.1875
- output_weight: bfloat16 [1024, 1024], P(('fsdp', 'expert')), may hold values from -0.75 to 0.75
- router_weight: bfloat16 [1024, 32], P(('fsdp', 'expert')), may hold values from -0.375 to 0.375
- attn_gain: bfloat16 [1024], P(('fsdp', 'expert')), may hold values from 0.5 to 1.5
- ffn_gain: bfloat16 [1024], P(('fsdp', 'expert')), may hold values from 0.5 to 1.5
- gate_weight: bfloat16 [32, 1024, 512], P('expert', 'fsdp'), may hold values from -0.1875 to 0.1875
- up_weight: bfloat16 [32, 1024, 512], P('expert', 'fsdp'), may hold values from -0.1875 to 0.1875
- down_weight: bfloat16 [32, 512, 1024], P('expert', 'fsdp'), may hold values from -0.75 to 0.75
- lengths: int32 [32, 2, 4], P(('fsdp', 'expert')), may hold values from 1 to 64, 128 in all within a row
- routes: int32 [8192, 8], P(('fsdp', 'expert')), may hold values from 0 to 31, all different within a row; in each aligned block of 128 rows (0 to 127, 128 to 255, ...) at most 40 rows name the same one
- cotangent: bfloat16 [8192, 1024], P(('fsdp', 'expert')), may hold values from -6 to 6
Outputs:
- layer_out: bfloat16 [8192, 1024], P(('fsdp', 'expert'))
- grad_tokens: float32 [8192, 1024], P(('fsdp', 'expert'))
- grad_query: float32 [1024, 1024], P(('fsdp', 'expert'))
- grad_key: float32 [1024, 512], P(('fsdp', 'expert'))
- grad_value: float32 [1024, 512], P(('fsdp', 'expert'))
- grad_output: float32 [1024, 1024], P(('fsdp', 'expert'))
- grad_router: float32 [1024, 32], P(('fsdp', 'expert'))
- grad_attn_gain: float32 [1024], P(('fsdp', 'expert'))
- grad_ffn_gain: float32 [1024], P(('fsdp', 'expert'))
- grad_gate: float32 [32, 1024, 512], P('expert', 'fsdp')
- grad_up: float32 [32, 1024, 512], P('expert', 'fsdp')
- grad_down: float32 [32, 512, 1024], P('expert', 'fsdp')
The draws below stay inside these ranges and needn't reach their ends.
Inputs may be any that keep to these rules, and one draw needn't show every extreme that they name: Each micro-batch of each device holds 4 sequences whose lengths sum to 128; the longest is exactly 64 tokens in every micro-batch. `routes`: the 8 experts of a row differ; in each aligned block of 128 rows (one micro-batch of one device) no expert is named by more than 40 rows, a bound that some block reaches.
All inputs are finite; a program needn't handle non-finite values.
Results may differ from the reference program's by a relative error of at most 0.015.
The reference program's roundings to bfloat16 on the way count: a program that leaves them out, or rounds other values in their place, can miss the bound.
Values may be sent and summed in bfloat16 or wider, within the bound.
No kernel may reach another device: no remote copies, remote signals or barrier semaphores. Data moves between devices by JAX's collectives and lax.ppermute only.
A program may use at most 256 MiB of HBM per device.

```python
import math
import jax
import jax.numpy as jnp
import numpy as np
from jax import lax

MODEL_WIDTH = 1024
QUERY_HEADS = 16
KEY_VALUE_HEADS = 8
HEAD_SIZE = 64
EXPERTS = 32
H_EXP = 512
TOPK = 8
DEVICE_TOKENS = 128
MB = 2
SEQ_MB = 4
LONGEST = 64
CAP = 40
TOKENS = 8192
N_FSDP = 16
N_EXPERT = 2


def shard_levels(own_key, extent, pieces, least, largest):
    gain, own = 1.0, jax.random.fold_in(own_key, 6)
    for position, shards_of in pieces:
        steps = jnp.exp(jax.random.uniform(jax.random.fold_in(own, position), (shards_of,), jnp.float32, least / len(pieces), largest / len(pieces)))
        gain = gain * jnp.repeat(steps, extent[position] // shards_of).reshape([-1 if axis == position else 1 for axis in range(len(extent))])
    return gain


def split_up(count, total, limit, slope):
    weights = [(1 << 20) // math.isqrt(grade ** slope) + 1 for grade in range(2, count + 1)]
    spare, holding = total - limit - (count - 1), [1] * (count - 1)
    while spare > 0:
        movable = [i for i in range(count - 1) if holding[i] < limit]
        pool, remaining = sum([weights[i] for i in movable]), spare
        for i in movable:
            addition = min(limit - holding[i], max(1, remaining * weights[i] // pool), spare)
            holding[i] = holding[i] + addition
            spare = spare - addition
    return np.array([limit] + holding)


def uneven(own_key, number_of, total, limit, slope):
    if number_of == 2:
        one = jax.random.randint(own_key, (), max(1, total - limit), min(limit, total - 1) + 1)
        return jnp.stack([one, total - one])
    sizes = jnp.asarray(split_up(number_of, total, limit, slope), jnp.int32)
    couples = (number_of - 1) // 2
    donor, taker = sizes[1:1 + 2 * couples:2], sizes[2:2 + 2 * couples:2]
    slack = jnp.minimum(donor - 1, limit - taker)
    passed = jax.random.randint(jax.random.fold_in(own_key, 1), (couples,), 0, 1 << 20) % (slack + 1)
    sizes = sizes.at[1:1 + 2 * couples:2].set(donor - passed).at[2:2 + 2 * couples:2].set(taker + passed)
    return sizes[jax.random.permutation(jax.random.fold_in(own_key, 2), number_of)]


def shared_out(key, own, number, rows, count, top, reach, skew):
    order = jax.random.permutation(key, count)
    heavy_load, common = portions_of(count, rows * top, reach, skew, True), portions_of(count, rows * top, reach, skew, False)
    places = jnp.arange(count)

    def named(sizes, rotation):
        used = int((sizes > 0).sum())
        fixed = max(1, used // 4)
        moved = fixed + (places - fixed + rotation * (used - fixed)) % max(1, count - fixed)
        return jnp.zeros((count,), jnp.int32).at[order[jnp.where(places < fixed, places, moved)]].set(jnp.asarray(sizes, jnp.int32))

    sizes = jnp.where(number % 4 == 0, named(heavy_load, number // 4), named(common, number - number // 4 - 1))
    mixed = jax.random.permutation(jax.random.fold_in(own, 3), count)
    giver, taker = mixed[0:count // 2 * 2:2], mixed[1:count // 2 * 2:2]
    room = jnp.minimum(sizes[giver] - 1, reach - sizes[taker]) // 2
    room = jnp.where((giver == order[0]) | (taker == order[0]) | (sizes[taker] == 0), 0, jnp.maximum(room, 0))
    moved = jax.random.randint(jax.random.fold_in(own, 4), (count // 2,), 0, 1 << 20) % (room + 1)
    sizes = sizes.at[giver].add(-moved).at[taker].add(moved)
    items = jnp.searchsorted(jnp.cumsum(sizes), jnp.arange(rows * top), side="right").astype(jnp.int32)
    table = items.reshape(top, rows).T
    table = table[jax.random.permutation(jax.random.fold_in(own, 1), rows)]
    rotation = jax.random.randint(jax.random.fold_in(own, 2), (rows, 1), 0, top)
    return jnp.take_along_axis(table, (jnp.arange(top)[None, :] + rotation) % top, axis=1)


def portions_of(number_of, total, reach, slope, full):
    weights = [(1 << 20) // math.isqrt(grade ** slope) + 1 for grade in range(1, number_of + 1)]
    largest = reach if full else min(reach, max(-(-total // number_of), total * weights[0] // sum(weights)))
    least = 1 if total - largest >= number_of - 1 else 0
    counts, spare = [largest] + [least] * (number_of - 1), total - largest - least * (number_of - 1)
    while spare > 0:
        candidates = [i for i in range(1, number_of) if counts[i] < largest] or [i for i in range(1, number_of) if counts[i] < reach]
        pool, left = sum([weights[i] for i in candidates]), spare
        for i in candidates:
            addition = min(reach - counts[i], max(1, left * weights[i] // pool), spare)
            counts[i] = counts[i] + addition
            spare = spare - addition
    return np.array(counts)


def centred(stream_key, extent, deviation, bound, cuts=(), held_as=jnp.bfloat16):
    array = jax.random.normal(stream_key, extent, jnp.float32) * deviation
    if len(cuts) > 0:
        array = shard_levels(stream_key, extent, cuts, -0.22, 0.18) * array
    return jnp.clip(array, min=-bound, max=bound).astype(held_as)


def setup_inputs(seed: int = 0) -> dict:
    arg_keys = jax.random.split(jax.random.key(seed), 15)
    tokens = centred(arg_keys[0], (TOKENS, MODEL_WIDTH), 1.0, 6.0, ((0, 32),))
    query_weight = centred(arg_keys[1], (MODEL_WIDTH, QUERY_HEADS * HEAD_SIZE), MODEL_WIDTH ** -0.5, 0.1875, ((0, 32),))
    key_projection = centred(arg_keys[2], (MODEL_WIDTH, KEY_VALUE_HEADS * HEAD_SIZE), MODEL_WIDTH ** -0.5, 0.1875, ((0, 32),))
    value_projection = centred(arg_keys[3], (MODEL_WIDTH, KEY_VALUE_HEADS * HEAD_SIZE), MODEL_WIDTH ** -0.5, 0.1875, ((0, 32),))
    output_weight = centred(arg_keys[4], (QUERY_HEADS * HEAD_SIZE, MODEL_WIDTH), (QUERY_HEADS * HEAD_SIZE // 16) ** -0.5, 0.75, ((0, 32),))
    router_weight = centred(arg_keys[5], (MODEL_WIDTH, EXPERTS), (MODEL_WIDTH // 4) ** -0.5, 0.375, ((0, 32),))
    attn_gain = jnp.clip(1.0 + 0.1 * jax.random.normal(arg_keys[6], (MODEL_WIDTH,), jnp.float32), 0.5, 1.5).astype(jnp.bfloat16)
    ffn_gain = jnp.clip(1.0 + 0.1 * jax.random.normal(arg_keys[7], (MODEL_WIDTH,), jnp.float32), 0.5, 1.5).astype(jnp.bfloat16)
    gate_weight = centred(arg_keys[8], (EXPERTS, MODEL_WIDTH, H_EXP), MODEL_WIDTH ** -0.5, 0.1875, ((0, 2), (1, 16)))
    up_weight = centred(arg_keys[9], (EXPERTS, MODEL_WIDTH, H_EXP), MODEL_WIDTH ** -0.5, 0.1875, ((0, 2), (1, 16)))
    down_weight = centred(arg_keys[10], (EXPERTS, H_EXP, MODEL_WIDTH), (H_EXP // 8) ** -0.5, 0.75, ((0, 2), (1, 16)))
    lengths = jax.vmap(lambda own: uneven(own, SEQ_MB, DEVICE_TOKENS, LONGEST, 2))(jax.random.split(arg_keys[11], (N_FSDP * N_EXPERT) * MB)).reshape((N_FSDP * N_EXPERT, MB, SEQ_MB)).astype(jnp.int32)
    routes_keys = jax.random.split(jax.random.fold_in(arg_keys[12], 1), TOKENS // DEVICE_TOKENS)
    routes_turns = jax.random.permutation(jax.random.fold_in(arg_keys[12], 3), TOKENS // DEVICE_TOKENS)
    routes = jax.vmap(lambda own, number: shared_out(jax.random.fold_in(arg_keys[12], 2), own, number, DEVICE_TOKENS, EXPERTS, TOPK, CAP, 1))(routes_keys, routes_turns).reshape((TOKENS, TOPK))
    cotangent = centred(arg_keys[13], (TOKENS, MODEL_WIDTH), 1.0, 6.0, ((0, 32),))
    return {"tokens": tokens, "query_weight": query_weight, "key_projection": key_projection, "value_projection": value_projection, "output_weight": output_weight, "router_weight": router_weight, "attn_gain": attn_gain, "ffn_gain": ffn_gain, "gate_weight": gate_weight, "up_weight": up_weight, "down_weight": down_weight, "lengths": lengths, "routes": routes, "cotangent": cotangent}


EPS = 1e-06
THETA = 10000.0
SCALE = 0.125
HIGH = lax.Precision.HIGHEST

@jax.custom_vjp
def lower_precision(v):
    return lax.optimization_barrier(v.astype(jnp.bfloat16)).astype(jnp.float32)

@jax.custom_vjp
def lower_precision_reverse(v):
    return v

def low_keep(v):
    return (lower_precision(v), None)

def low_pass(kept, grad):
    return (grad,)

def back_keep(v):
    return (v, None)

def back_low(kept, grad):
    return (lower_precision(grad),)
lower_precision.defvjp(low_keep, low_pass)
lower_precision_reverse.defvjp(back_keep, back_low)

def product_highest(left, right):
    return jnp.dot(left, right, precision=HIGH, preferred_element_type=jnp.float32)

def sequence_layout(seq_lengths, row_number):
    row_index = jnp.arange(row_number, dtype=jnp.int32)
    seq_ends = jnp.cumsum(seq_lengths).astype(jnp.int32)
    starts = (seq_ends - seq_lengths).astype(jnp.int32)
    member = ((row_index[:, None] >= starts[None, :]) & (row_index[:, None] < seq_ends[None, :])).astype(jnp.int32)
    labels = jnp.arange(seq_lengths.shape[0], dtype=jnp.int32)
    segment = lax.optimization_barrier(jnp.sum(member * labels[None, :], axis=1)).astype(jnp.int32)
    offset = lax.optimization_barrier(jnp.sum(member * starts[None, :], axis=1)).astype(jnp.int32)
    return (segment, row_index - offset)

def rotary_apply(values, token_positions, reverse):
    half_width = values.shape[-1] // 2
    frequency = THETA ** (-2.0 * jnp.arange(half_width, dtype=jnp.float32) / values.shape[-1])
    angles = token_positions.astype(jnp.float32)[:, None] * frequency[None, :]
    cosine = jnp.cos(angles)[:, None, :]
    sine_part = jnp.sin(angles)[:, None, :]
    if reverse:
        sine_part = -sine_part
    first_half = values[..., :half_width]
    second_half = values[..., half_width:]
    return jnp.concatenate([first_half * cosine - second_half * sine_part, second_half * cosine + first_half * sine_part], axis=-1)

def attend_heads(block):
    query_rows, key_matrix_rows, value_matrix_rows, seq_lengths = block
    row_number = query_rows.shape[0]
    segment, token_positions = sequence_layout(seq_lengths, row_number)
    row_index = jnp.arange(row_number, dtype=jnp.int32)
    allowed = (segment[:, None] == segment[None, :]) & (row_index[:, None] >= row_index[None, :])
    query_grouped = query_rows.reshape(row_number, KEY_VALUE_HEADS, QUERY_HEADS // KEY_VALUE_HEADS, HEAD_SIZE)
    scores = lower_precision_reverse(jnp.einsum('qgrd,kgd->grqk', query_grouped, key_matrix_rows, precision=HIGH) * SCALE)
    scores = jnp.where(allowed, scores, -1e+30)
    row_max = lax.optimization_barrier(jnp.max(scores, axis=-1, keepdims=True))
    exp_scores = jnp.exp(scores - row_max)
    attn_probs = lower_precision(exp_scores / lax.optimization_barrier(jnp.sum(exp_scores, axis=-1, keepdims=True)))
    attention_mixed = jnp.einsum('grqk,kgd->qgrd', attn_probs, value_matrix_rows, precision=HIGH)
    return attention_mixed.reshape(row_number, QUERY_HEADS * HEAD_SIZE)

def forward(tokens, query_weight, key_projection, value_projection, output_weight, router_weight, attn_gain, ffn_gain, gate_weight, up_weight, down_weight, lengths, slot_table, routes):
    block_list = lengths.reshape(-1, SEQ_MB)
    block_total = block_list.shape[0]
    token_number = tokens.shape[0]
    token_positions = jax.vmap(lambda seq_lengths: sequence_layout(seq_lengths, DEVICE_TOKENS)[1])(block_list).reshape(-1)
    attention_input = lower_precision(tokens * lax.rsqrt(lax.optimization_barrier(jnp.mean(tokens * tokens, axis=1, keepdims=True)) + EPS) * attn_gain)
    query_rows = lower_precision(rotary_apply(lower_precision_reverse(product_highest(attention_input, query_weight)).reshape(token_number, QUERY_HEADS, HEAD_SIZE), token_positions, False))
    key_matrix_rows = lower_precision(rotary_apply(lower_precision_reverse(product_highest(attention_input, key_projection)).reshape(token_number, KEY_VALUE_HEADS, HEAD_SIZE), token_positions, False))
    value_matrix_rows = lower_precision_reverse(lower_precision(product_highest(attention_input, value_projection))).reshape(token_number, KEY_VALUE_HEADS, HEAD_SIZE)
    attention_mixed = lax.map(jax.checkpoint(attend_heads), (query_rows.reshape(block_total, DEVICE_TOKENS, QUERY_HEADS, HEAD_SIZE), key_matrix_rows.reshape(block_total, DEVICE_TOKENS, KEY_VALUE_HEADS, HEAD_SIZE), value_matrix_rows.reshape(block_total, DEVICE_TOKENS, KEY_VALUE_HEADS, HEAD_SIZE), block_list))
    attention_mixed = lower_precision_reverse(lower_precision(attention_mixed.reshape(token_number, QUERY_HEADS * HEAD_SIZE)))
    middle = tokens + lower_precision_reverse(product_highest(attention_mixed, output_weight))
    ffn_in = lower_precision(middle * lax.rsqrt(lax.optimization_barrier(jnp.mean(middle * middle, axis=1, keepdims=True)) + EPS) * ffn_gain)
    logits = product_highest(ffn_in, router_weight)
    gate_probs = jax.nn.softmax(jnp.take_along_axis(logits, routes, axis=1), axis=1)
    padded_in = jnp.concatenate([ffn_in, jnp.zeros((1, MODEL_WIDTH), jnp.float32)], axis=0)
    padded_gates = jnp.concatenate([gate_probs.reshape(-1), jnp.zeros((1,), jnp.float32)], axis=0)

    def expert_step(running, item):
        slot_rows, gate_matrix, up_matrix, down_matrix = item
        token_rows = slot_rows // TOPK
        inputs = lower_precision_reverse(padded_in[token_rows])
        gate_act = lower_precision_reverse(product_highest(inputs, gate_matrix))
        up_act = lower_precision_reverse(product_highest(inputs, up_matrix))
        hidden = lower_precision(jax.nn.silu(gate_act) * up_act)
        produced = lower_precision_reverse(lower_precision(product_highest(hidden, down_matrix)))
        running = running.at[token_rows].add(produced * padded_gates[slot_rows][:, None])
        return (running, None)
    combined, unused = lax.scan(jax.checkpoint(expert_step), jnp.zeros((token_number + 1, MODEL_WIDTH), jnp.float32), (slot_table, gate_weight, up_weight, down_weight))
    return middle + combined[:token_number]

def reference(tokens, query_weight, key_projection, value_projection, output_weight, router_weight, attn_gain, ffn_gain, gate_weight, up_weight, down_weight, lengths, routes, cotangent):
    block_total = tokens.shape[0] // DEVICE_TOKENS
    blocked = routes.reshape(block_total, DEVICE_TOKENS, TOPK)
    chosen = (blocked[:, :, :, None] == jnp.arange(EXPERTS, dtype=jnp.int32)[None, None, None, :]).astype(jnp.int32)
    expert_hits = lax.optimization_barrier(jnp.sum(chosen, axis=2))
    before = (jnp.cumsum(expert_hits, axis=1) - expert_hits).astype(jnp.int32)
    slot_rank = lax.optimization_barrier(jnp.sum(chosen * before[:, :, None, :], axis=3)).astype(jnp.int32)
    columns = (jnp.arange(block_total, dtype=jnp.int32)[:, None, None] * CAP + slot_rank).reshape(-1).astype(jnp.int32)
    entries = block_total * DEVICE_TOKENS * TOPK
    slot_table = jnp.full((EXPERTS, block_total * CAP), entries, jnp.int32)
    slot_table = slot_table.at[routes.reshape(-1), columns].set(jnp.arange(entries, dtype=jnp.int32))
    floats = tuple((array_in.astype(jnp.float32) for array_in in (tokens, query_weight, key_projection, value_projection, output_weight, router_weight, attn_gain, ffn_gain, gate_weight, up_weight, down_weight)))

    def layer(*weights_in):
        return forward(*weights_in, lengths, slot_table, routes)
    output, pull_back = jax.vjp(layer, *floats)
    grads = pull_back(cotangent.astype(jnp.float32))
    return (output.astype(jnp.bfloat16), grads[0], grads[1], grads[2], grads[3], grads[4], grads[5], grads[6], grads[7], grads[8], grads[9], grads[10])
```

```python
import jax
import jax.numpy as jnp
from jax import lax
from jax.sharding import PartitionSpec as P

MODEL_WIDTH = 1024
QUERY_HEADS = 16
KEY_VALUE_HEADS = 8
HEAD_SIZE = 64
EXPERTS = 32
DEVICE_TOKENS = 128
MB = 2
CAP = 40
ROWS = MB * DEVICE_TOKENS
SLOTS = MB * CAP
Q_COLS = QUERY_HEADS * HEAD_SIZE
KV_COLS = KEY_VALUE_HEADS * HEAD_SIZE
QKV_COLS = Q_COLS + 2 * KV_COLS
SMALL_COLS = 128

EPS = 1e-06
THETA = 10000.0
SCALE = 0.125
HIGH = lax.Precision.HIGHEST
BOTH = ("fsdp", "expert")
F32 = jnp.float32
BF16 = jnp.bfloat16


def mm(spec, a, b):
    return jnp.einsum(spec, a, b, preferred_element_type=F32)


def sequence_layout(seq_lengths, row_number):
    row_index = jnp.arange(row_number, dtype=jnp.int32)
    seq_ends = jnp.cumsum(seq_lengths)
    starts = seq_ends - seq_lengths
    member = (
        (row_index[:, None] >= starts[None, :]) & (row_index[:, None] < seq_ends[None, :])
    ).astype(jnp.int32)
    labels = jnp.arange(seq_lengths.shape[0], dtype=jnp.int32)
    segment = jnp.sum(member * labels[None, :], axis=1)
    offset = jnp.sum(member * starts[None, :], axis=1)
    return (segment, row_index - offset)


def rotary_tables(token_positions):
    half_width = HEAD_SIZE // 2
    frequency = THETA ** (-2.0 * jnp.arange(half_width, dtype=F32) / HEAD_SIZE)
    angles = token_positions.astype(F32)[:, None] * frequency[None, :]
    return jnp.cos(angles)[:, None, :], jnp.sin(angles)[:, None, :]


def rotary_apply(values, cosine, sine_part):
    half_width = HEAD_SIZE // 2
    first_half = values[..., :half_width]
    second_half = values[..., half_width:]
    return jnp.concatenate(
        [
            first_half * cosine - second_half * sine_part,
            second_half * cosine + first_half * sine_part,
        ],
        axis=-1,
    )


def rms_scale(values):
    return lax.rsqrt(jnp.mean(values * values, axis=1, keepdims=True) + EPS)


def norm_back(grad_normed, gain_vec, plain_part, scale_part):
    grad_gain = jnp.sum(grad_normed * plain_part, axis=0)
    shaped = grad_normed * gain_vec[None, :]
    grad_input = scale_part * (
        shaped - plain_part * jnp.mean(shaped * plain_part, axis=1, keepdims=True)
    )
    return (grad_input, grad_gain)


def fsdp_groups(local_experts):
    size = lax.axis_size("fsdp")
    runs = size // local_experts
    if runs == 1:
        return None, None
    inner = [[s * local_experts + j for j in range(local_experts)] for s in range(runs)]
    cross = [[s * local_experts + j for s in range(runs)] for j in range(local_experts)]
    return inner, cross


def weight_to_expert(weight, inner, cross):
    part = lax.all_to_all(
        weight, "fsdp", split_axis=0, concat_axis=1, axis_index_groups=inner, tiled=True
    )[0]
    if cross is not None:
        part = lax.all_gather(part, "fsdp", axis=0, axis_index_groups=cross, tiled=True)
    return part


def grad_to_owners(grad, inner, cross):
    if cross is not None:
        grad = lax.psum_scatter(
            grad, "fsdp", scatter_dimension=0, axis_index_groups=cross, tiled=True
        )
    return lax.all_to_all(
        grad.astype(BF16)[None],
        "fsdp",
        split_axis=1,
        concat_axis=0,
        axis_index_groups=inner,
        tiled=True,
    ).astype(F32)


def exchange(rows, local_experts, inner):
    if inner is None:
        return lax.all_to_all(rows, BOTH, split_axis=0, concat_axis=0, tiled=True)
    groups = EXPERTS // local_experts
    shaped = rows.reshape((local_experts, groups) + rows.shape[1:])
    shaped = lax.all_to_all(
        shaped, "fsdp", split_axis=0, concat_axis=0, axis_index_groups=inner, tiled=True
    )
    shaped = lax.all_to_all(shaped, "expert", split_axis=1, concat_axis=1, tiled=True)
    return shaped.reshape(rows.shape)


def per_device(
    tokens,
    query_weight,
    key_projection,
    value_projection,
    output_weight,
    router_weight,
    attn_gain,
    ffn_gain,
    gate_weight,
    up_weight,
    down_weight,
    lengths,
    routes,
    cotangent,
):
    local_experts = gate_weight.shape[0]
    groups = EXPERTS // local_experts
    inner, cross = fsdp_groups(local_experts)
    heads = QUERY_HEADS // KEY_VALUE_HEADS

    small = jnp.concatenate(
        [
            router_weight,
            attn_gain[:, None],
            ffn_gain[:, None],
            jnp.zeros((router_weight.shape[0], SMALL_COLS - EXPERTS - 2), BF16),
        ],
        axis=1,
    )
    packed = jnp.concatenate(
        [query_weight, key_projection, value_projection, output_weight, small], axis=1
    )
    full = lax.all_gather(packed, BOTH, axis=0, tiled=True)
    qkv_full = full[:, :QKV_COLS]
    o_full = full[:, QKV_COLS : QKV_COLS + MODEL_WIDTH]
    small_full = full[:, QKV_COLS + MODEL_WIDTH :]
    r_full = small_full[:, :EXPERTS]
    gain_one = small_full[:, EXPERTS].astype(F32)
    gain_two = small_full[:, EXPERTS + 1].astype(F32)
    gate_full = weight_to_expert(gate_weight, inner, cross)
    up_full = weight_to_expert(up_weight, inner, cross)
    down_full = weight_to_expert(down_weight, inner, cross)

    plain_in = tokens.astype(F32)
    grad_out = cotangent.astype(F32)
    layouts = [sequence_layout(lengths[0, b], DEVICE_TOKENS) for b in range(MB)]
    segment = jnp.stack([s for s, _ in layouts])
    cosine, sine = rotary_tables(jnp.concatenate([p for _, p in layouts]))
    row_index = jnp.arange(DEVICE_TOKENS, dtype=jnp.int32)
    allowed = (segment[:, :, None] == segment[:, None, :]) & (
        row_index[:, None] >= row_index[None, :]
    )[None]

    local = jnp.arange(EXPERTS, dtype=jnp.int32)
    named = (local % groups) * local_experts + local // groups
    hits = jnp.any(routes[:, :, None] == named[None, None, :], axis=1)
    all_rows = jnp.arange(ROWS, dtype=jnp.int32)
    below = (all_rows[:, None] > all_rows[None, :]).astype(BF16)
    rank = mm("ts,se->te", below, hits.astype(BF16)).astype(jnp.int32)
    rank = jnp.where(hits, rank, -1)
    slot_id = jnp.arange(SLOTS, dtype=jnp.int32)
    place = rank.T[:, None, :] == slot_id[None, :, None]
    place_rows = place.astype(BF16).reshape(EXPERTS * SLOTS, ROWS)

    scale_one = rms_scale(plain_in)
    plain_one = plain_in * scale_one
    attention_input = (plain_one * gain_one[None, :]).astype(BF16)
    qkv = mm("td,de->te", attention_input, qkv_full)
    query = (
        rotary_apply(qkv[:, :Q_COLS].reshape(ROWS, QUERY_HEADS, HEAD_SIZE), cosine, sine)
        .astype(BF16)
        .reshape(MB, DEVICE_TOKENS, KEY_VALUE_HEADS, heads, HEAD_SIZE)
    )
    key = (
        rotary_apply(
            qkv[:, Q_COLS : Q_COLS + KV_COLS].reshape(ROWS, KEY_VALUE_HEADS, HEAD_SIZE),
            cosine,
            sine,
        )
        .astype(BF16)
        .reshape(MB, DEVICE_TOKENS, KEY_VALUE_HEADS, HEAD_SIZE)
    )
    value = (
        qkv[:, Q_COLS + KV_COLS :]
        .astype(BF16)
        .reshape(MB, DEVICE_TOKENS, KEY_VALUE_HEADS, HEAD_SIZE)
    )
    scores = mm("bqgrd,bkgd->bgrqk", query, key) * SCALE
    scores = jnp.where(allowed[:, None, None], scores, -1e30)
    exp_scores = jnp.exp(scores - jnp.max(scores, axis=-1, keepdims=True))
    probs = exp_scores / jnp.sum(exp_scores, axis=-1, keepdims=True)
    probs_low = probs.astype(BF16)
    mixed = mm("bgrqk,bkgd->bqgrd", probs_low, value).reshape(ROWS, Q_COLS).astype(BF16)
    middle = plain_in + mm("te,ed->td", mixed, o_full)
    scale_two = rms_scale(middle)
    plain_two = middle * scale_two
    ffn_in = (plain_two * gain_two[None, :]).astype(BF16)

    dispatch = mm("st,td->sd", place_rows, ffn_in).astype(BF16)
    received = exchange(
        dispatch.reshape(EXPERTS, SLOTS, MODEL_WIDTH), local_experts, inner
    ).reshape(EXPERTS * SLOTS, MODEL_WIDTH)

    logits = mm("td,de->te", ffn_in, r_full)
    logits = logits.reshape(ROWS, groups, local_experts).swapaxes(1, 2).reshape(ROWS, EXPERTS)
    logits = jnp.where(hits, logits, -jnp.inf)
    exp_logits = jnp.exp(logits - jnp.max(logits, axis=1, keepdims=True))
    gates = exp_logits / jnp.sum(exp_logits, axis=1, keepdims=True)
    slot_gates = jnp.sum(jnp.where(place, gates.T[:, None, :], 0.0), axis=2)

    cot_rows = mm("st,td->sd", place_rows, cotangent).reshape(EXPERTS, SLOTS, MODEL_WIDTH)
    grad_recv = exchange(
        (slot_gates[:, :, None] * cot_rows).astype(BF16), local_experts, inner
    ).reshape(EXPERTS * SLOTS, MODEL_WIDTH)

    gate_act = mm("sd,dh->sh", received, gate_full)
    up_act = mm("sd,dh->sh", received, up_full)
    sigmoid_g = jax.nn.sigmoid(gate_act)
    silu_gate = gate_act * sigmoid_g
    hidden = (silu_gate * up_act).astype(BF16)
    produced = mm("sh,hd->sd", hidden, down_full).astype(BF16)
    returned = exchange(
        produced.reshape(EXPERTS, SLOTS, MODEL_WIDTH), local_experts, inner
    ).reshape(EXPERTS * SLOTS, MODEL_WIDTH)

    grad_hidden = mm("sd,hd->sh", grad_recv, down_full)
    grad_gact = (
        grad_hidden * up_act * sigmoid_g * (1.0 + gate_act * (1.0 - sigmoid_g))
    ).astype(BF16)
    grad_uact = (grad_hidden * silu_gate).astype(BF16)
    grad_inputs = (
        mm("sh,dh->sd", grad_gact, gate_full) + mm("sh,dh->sd", grad_uact, up_full)
    ).astype(BF16)
    grad_back = exchange(
        grad_inputs.reshape(EXPERTS, SLOTS, MODEL_WIDTH), local_experts, inner
    ).reshape(EXPERTS * SLOTS, MODEL_WIDTH)
    grad_down = grad_to_owners(mm("sh,sd->hd", hidden, grad_recv), inner, cross)
    grad_gate = grad_to_owners(mm("sd,sh->dh", received, grad_gact), inner, cross)
    grad_up = grad_to_owners(mm("sd,sh->dh", received, grad_uact), inner, cross)

    slot_column = slot_gates.reshape(EXPERTS * SLOTS, 1)
    part_one = slot_column.astype(BF16)
    rest = slot_column - part_one.astype(F32)
    part_two = rest.astype(BF16)
    part_three = (rest - part_two.astype(F32)).astype(BF16)
    combined = (
        mm("st,sd->td", place_rows * part_three, returned)
        + mm("st,sd->td", place_rows * part_two, returned)
    ) + mm("st,sd->td", place_rows * part_one, returned)
    layer_out = (middle + combined).astype(BF16)

    products = mm("sd,td->st", returned, cotangent).reshape(EXPERTS, SLOTS, ROWS)
    grad_gates = jnp.sum(jnp.where(place, products, 0.0), axis=1).T
    grad_logits = gates * (grad_gates - jnp.sum(gates * grad_gates, axis=1, keepdims=True))
    grad_logits = (
        grad_logits.reshape(ROWS, local_experts, groups).swapaxes(1, 2).reshape(ROWS, EXPERTS)
    )
    grad_router = jnp.dot(ffn_in.astype(F32).T, grad_logits, precision=HIGH)
    grad_ffn_in = jnp.dot(grad_logits, r_full.astype(F32).T, precision=HIGH)
    grad_ffn_in = grad_ffn_in + mm("st,sd->td", place_rows, grad_back)
    grad_middle, grad_gain_two = norm_back(grad_ffn_in, gain_two, plain_two, scale_two)
    grad_middle = grad_middle + grad_out
    grad_attn = grad_middle.astype(BF16)
    grad_o = lax.psum_scatter(
        mm("te,td->ed", mixed, grad_attn), BOTH, scatter_dimension=0, tiled=True
    )
    grad_mix = (
        mm("td,ed->te", grad_attn, o_full)
        .astype(BF16)
        .reshape(MB, DEVICE_TOKENS, KEY_VALUE_HEADS, heads, HEAD_SIZE)
    )
    grad_value = mm("bgrqk,bqgrd->bkgd", probs_low, grad_mix).astype(BF16).reshape(ROWS, KV_COLS)
    grad_probs = mm("bqgrd,bkgd->bgrqk", grad_mix, value)
    row_inner = jnp.sum(probs * grad_probs, axis=-1, keepdims=True)
    grad_scores = (probs * (grad_probs - row_inner)).astype(BF16)
    grad_query = mm("bgrqk,bkgd->bqgrd", grad_scores, key) * SCALE
    grad_query = (
        rotary_apply(grad_query.reshape(ROWS, QUERY_HEADS, HEAD_SIZE), cosine, -sine)
        .astype(BF16)
        .reshape(ROWS, Q_COLS)
    )
    grad_key = mm("bgrqk,bqgrd->bkgd", grad_scores, query) * SCALE
    grad_key = (
        rotary_apply(grad_key.reshape(ROWS, KEY_VALUE_HEADS, HEAD_SIZE), cosine, -sine)
        .astype(BF16)
        .reshape(ROWS, KV_COLS)
    )
    grad_qkv = jnp.concatenate([grad_query, grad_key, grad_value], axis=1)
    grad_qkv_w = lax.psum_scatter(
        mm("td,te->de", attention_input, grad_qkv), BOTH, scatter_dimension=0, tiled=True
    )
    grad_attn_in = mm("te,de->td", grad_qkv, qkv_full)
    grad_plain, grad_gain_one = norm_back(grad_attn_in, gain_one, plain_one, scale_one)
    small_grads = jnp.concatenate(
        [
            grad_router,
            grad_gain_one[:, None],
            grad_gain_two[:, None],
            jnp.zeros((MODEL_WIDTH, SMALL_COLS - EXPERTS - 2), F32),
        ],
        axis=1,
    )
    small_owned = lax.psum_scatter(small_grads, BOTH, scatter_dimension=0, tiled=True)
    return (
        layer_out,
        grad_plain + grad_middle,
        grad_qkv_w[:, :Q_COLS],
        grad_qkv_w[:, Q_COLS : Q_COLS + KV_COLS],
        grad_qkv_w[:, Q_COLS + KV_COLS :],
        grad_o,
        small_owned[:, :EXPERTS],
        small_owned[:, EXPERTS],
        small_owned[:, EXPERTS + 1],
        grad_gate,
        grad_up,
        grad_down,
    )


def solution(mesh):
    in_specs = (
        P(("fsdp", "expert"), None),
        P(("fsdp", "expert"), None),
        P(("fsdp", "expert"), None),
        P(("fsdp", "expert"), None),
        P(("fsdp", "expert"), None),
        P(("fsdp", "expert"), None),
        P(("fsdp", "expert")),
        P(("fsdp", "expert")),
        P("expert", "fsdp", None),
        P("expert", "fsdp", None),
        P("expert", "fsdp", None),
        P(("fsdp", "expert"), None, None),
        P(("fsdp", "expert"), None),
        P(("fsdp", "expert"), None),
    )
    out_specs = (
        P(("fsdp", "expert"), None),
        P(("fsdp", "expert"), None),
        P(("fsdp", "expert"), None),
        P(("fsdp", "expert"), None),
        P(("fsdp", "expert"), None),
        P(("fsdp", "expert"), None),
        P(("fsdp", "expert"), None),
        P(("fsdp", "expert")),
        P(("fsdp", "expert")),
        P("expert", "fsdp", None),
        P("expert", "fsdp", None),
        P("expert", "fsdp", None),
    )
    return jax.shard_map(
        per_device, mesh=mesh, in_specs=in_specs, out_specs=out_specs, check_vma=False
    )
```

```python
import jax
import jax.numpy as jnp
from jax import lax
from jax.sharding import PartitionSpec as P

MODEL_WIDTH = 1024
QUERY_HEADS = 16
KEY_VALUE_HEADS = 8
HEAD_SIZE = 64
EXPERTS = 32
DEVICE_TOKENS = 128
MB = 2
CAP = 40
ROWS = MB * DEVICE_TOKENS
SLOTS = MB * CAP
Q_COLS = QUERY_HEADS * HEAD_SIZE
KV_COLS = KEY_VALUE_HEADS * HEAD_SIZE
QKV_COLS = Q_COLS + 2 * KV_COLS
SMALL_COLS = 128

EPS = 1e-06
THETA = 10000.0
SCALE = 0.125
HIGH = lax.Precision.HIGHEST
BOTH = ("fsdp", "expert")
F32 = jnp.float32
BF16 = jnp.bfloat16


def mm(spec, a, b):
    return jnp.einsum(spec, a, b, preferred_element_type=F32)


def sequence_layout(seq_lengths, row_number):
    row_index = jnp.arange(row_number, dtype=jnp.int32)
    seq_ends = jnp.cumsum(seq_lengths)
    starts = seq_ends - seq_lengths
    member = (
        (row_index[:, None] >= starts[None, :]) & (row_index[:, None] < seq_ends[None, :])
    ).astype(jnp.int32)
    labels = jnp.arange(seq_lengths.shape[0], dtype=jnp.int32)
    segment = jnp.sum(member * labels[None, :], axis=1)
    offset = jnp.sum(member * starts[None, :], axis=1)
    return (segment, row_index - offset)


def rotary_tables(token_positions):
    half_width = HEAD_SIZE // 2
    frequency = THETA ** (-2.0 * jnp.arange(half_width, dtype=F32) / HEAD_SIZE)
    angles = token_positions.astype(F32)[:, None] * frequency[None, :]
    return jnp.cos(angles)[:, None, :], jnp.sin(angles)[:, None, :]


def rotary_apply(values, cosine, sine_part):
    half_width = HEAD_SIZE // 2
    first_half = values[..., :half_width]
    second_half = values[..., half_width:]
    return jnp.concatenate(
        [
            first_half * cosine - second_half * sine_part,
            second_half * cosine + first_half * sine_part,
        ],
        axis=-1,
    )


def rms_scale(values):
    return lax.rsqrt(jnp.mean(values * values, axis=1, keepdims=True) + EPS)


def norm_back(grad_normed, gain_vec, plain_part, scale_part):
    grad_gain = jnp.sum(grad_normed * plain_part, axis=0)
    shaped = grad_normed * gain_vec[None, :]
    grad_input = scale_part * (
        shaped - plain_part * jnp.mean(shaped * plain_part, axis=1, keepdims=True)
    )
    return (grad_input, grad_gain)


def fsdp_groups(local_experts):
    size = lax.axis_size("fsdp")
    runs = size // local_experts
    if runs == 1:
        return None, None
    inner = [[s * local_experts + j for j in range(local_experts)] for s in range(runs)]
    cross = [[s * local_experts + j for s in range(runs)] for j in range(local_experts)]
    return inner, cross


def weight_to_expert(weight, inner, cross):
    part = lax.all_to_all(
        weight, "fsdp", split_axis=0, concat_axis=1, axis_index_groups=inner, tiled=True
    )[0]
    if cross is not None:
        part = lax.all_gather(part, "fsdp", axis=0, axis_index_groups=cross, tiled=True)
    return part


def grad_to_owners(grad, inner, cross):
    if cross is not None:
        grad = lax.psum_scatter(
            grad, "fsdp", scatter_dimension=0, axis_index_groups=cross, tiled=True
        )
    return lax.all_to_all(
        grad.astype(BF16)[None],
        "fsdp",
        split_axis=1,
        concat_axis=0,
        axis_index_groups=inner,
        tiled=True,
    ).astype(F32)


def exchange(rows, local_experts, inner):
    if inner is None:
        return lax.all_to_all(rows, BOTH, split_axis=0, concat_axis=0, tiled=True)
    groups = EXPERTS // local_experts
    shaped = rows.reshape((local_experts, groups) + rows.shape[1:])
    shaped = lax.all_to_all(
        shaped, "fsdp", split_axis=0, concat_axis=0, axis_index_groups=inner, tiled=True
    )
    shaped = lax.all_to_all(shaped, "expert", split_axis=1, concat_axis=1, tiled=True)
    return shaped.reshape(rows.shape)


def sum_to_owners(grad):
    devices = lax.axis_size(BOTH)
    parts = grad.reshape(devices, grad.shape[0] // devices, grad.shape[1])
    parts = lax.all_to_all(parts, BOTH, split_axis=0, concat_axis=0, tiled=True)
    return jnp.sum(parts.astype(F32), axis=0)


def per_device(
    tokens,
    query_weight,
    key_projection,
    value_projection,
    output_weight,
    router_weight,
    attn_gain,
    ffn_gain,
    gate_weight,
    up_weight,
    down_weight,
    lengths,
    routes,
    cotangent,
):
    local_experts = gate_weight.shape[0]
    groups = EXPERTS // local_experts
    inner, cross = fsdp_groups(local_experts)
    heads = QUERY_HEADS // KEY_VALUE_HEADS

    small = jnp.concatenate(
        [
            router_weight,
            attn_gain[:, None],
            ffn_gain[:, None],
            jnp.zeros((router_weight.shape[0], SMALL_COLS - EXPERTS - 2), BF16),
        ],
        axis=1,
    )
    packed = jnp.concatenate(
        [query_weight, key_projection, value_projection, output_weight, small], axis=1
    )
    full = lax.all_gather(packed, BOTH, axis=0, tiled=True)
    qkv_full = full[:, :QKV_COLS]
    o_full = full[:, QKV_COLS : QKV_COLS + MODEL_WIDTH]
    small_full = full[:, QKV_COLS + MODEL_WIDTH :]
    r_full = small_full[:, :EXPERTS]
    gain_one = small_full[:, EXPERTS].astype(F32)
    gain_two = small_full[:, EXPERTS + 1].astype(F32)
    gate_full = weight_to_expert(gate_weight, inner, cross)
    up_full = weight_to_expert(up_weight, inner, cross)
    down_full = weight_to_expert(down_weight, inner, cross)

    plain_in = tokens.astype(F32)
    grad_out = cotangent.astype(F32)
    layouts = [sequence_layout(lengths[0, b], DEVICE_TOKENS) for b in range(MB)]
    segment = jnp.stack([s for s, _ in layouts])
    cosine, sine = rotary_tables(jnp.concatenate([p for _, p in layouts]))
    row_index = jnp.arange(DEVICE_TOKENS, dtype=jnp.int32)
    allowed = (segment[:, :, None] == segment[:, None, :]) & (
        row_index[:, None] >= row_index[None, :]
    )[None]

    local = jnp.arange(EXPERTS, dtype=jnp.int32)
    named = (local % groups) * local_experts + local // groups
    hits = jnp.any(routes[:, :, None] == named[None, None, :], axis=1)
    all_rows = jnp.arange(ROWS, dtype=jnp.int32)
    below = (all_rows[:, None] > all_rows[None, :]).astype(BF16)
    rank = mm("ts,se->te", below, hits.astype(BF16)).astype(jnp.int32)
    rank = jnp.where(hits, rank, -1)
    slot_id = jnp.arange(SLOTS, dtype=jnp.int32)
    place = rank.T[:, None, :] == slot_id[None, :, None]
    place_rows = place.astype(BF16).reshape(EXPERTS * SLOTS, ROWS)

    scale_one = rms_scale(plain_in)
    plain_one = plain_in * scale_one
    attention_input = (plain_one * gain_one[None, :]).astype(BF16)
    qkv = mm("td,de->te", attention_input, qkv_full)
    query = (
        rotary_apply(qkv[:, :Q_COLS].reshape(ROWS, QUERY_HEADS, HEAD_SIZE), cosine, sine)
        .astype(BF16)
        .reshape(MB, DEVICE_TOKENS, KEY_VALUE_HEADS, heads, HEAD_SIZE)
    )
    key = (
        rotary_apply(
            qkv[:, Q_COLS : Q_COLS + KV_COLS].reshape(ROWS, KEY_VALUE_HEADS, HEAD_SIZE),
            cosine,
            sine,
        )
        .astype(BF16)
        .reshape(MB, DEVICE_TOKENS, KEY_VALUE_HEADS, HEAD_SIZE)
    )
    value = (
        qkv[:, Q_COLS + KV_COLS :]
        .astype(BF16)
        .reshape(MB, DEVICE_TOKENS, KEY_VALUE_HEADS, HEAD_SIZE)
    )
    scores = mm("bqgrd,bkgd->bgrqk", query, key) * SCALE
    scores = jnp.where(allowed[:, None, None], scores, -1e30)
    exp_scores = jnp.exp(scores - jnp.max(scores, axis=-1, keepdims=True))
    probs = exp_scores / jnp.sum(exp_scores, axis=-1, keepdims=True)
    probs_low = probs.astype(BF16)
    mixed = mm("bgrqk,bkgd->bqgrd", probs_low, value).reshape(ROWS, Q_COLS).astype(BF16)
    middle = plain_in + mm("te,ed->td", mixed, o_full)
    scale_two = rms_scale(middle)
    plain_two = middle * scale_two
    ffn_in = (plain_two * gain_two[None, :]).astype(BF16)

    dispatch = mm("st,td->sd", place_rows, ffn_in).astype(BF16)
    received = exchange(
        dispatch.reshape(EXPERTS, SLOTS, MODEL_WIDTH), local_experts, inner
    ).reshape(EXPERTS * SLOTS, MODEL_WIDTH)

    logits = mm("td,de->te", ffn_in, r_full)
    logits = logits.reshape(ROWS, groups, local_experts).swapaxes(1, 2).reshape(ROWS, EXPERTS)
    logits = jnp.where(hits, logits, -jnp.inf)
    exp_logits = jnp.exp(logits - jnp.max(logits, axis=1, keepdims=True))
    gates = exp_logits / jnp.sum(exp_logits, axis=1, keepdims=True)
    slot_gates = jnp.sum(jnp.where(place, gates.T[:, None, :], 0.0), axis=2)

    cot_rows = mm("st,td->sd", place_rows, cotangent).reshape(EXPERTS, SLOTS, MODEL_WIDTH)
    grad_recv = exchange(
        (slot_gates[:, :, None] * cot_rows).astype(BF16), local_experts, inner
    ).reshape(EXPERTS * SLOTS, MODEL_WIDTH)

    gate_act = mm("sd,dh->sh", received, gate_full)
    up_act = mm("sd,dh->sh", received, up_full)
    sigmoid_g = jax.nn.sigmoid(gate_act)
    silu_gate = gate_act * sigmoid_g
    hidden = (silu_gate * up_act).astype(BF16)
    produced = mm("sh,hd->sd", hidden, down_full).astype(BF16)
    returned = exchange(
        produced.reshape(EXPERTS, SLOTS, MODEL_WIDTH), local_experts, inner
    ).reshape(EXPERTS * SLOTS, MODEL_WIDTH)

    grad_hidden = mm("sd,hd->sh", grad_recv, down_full)
    grad_gact = (
        grad_hidden * up_act * sigmoid_g * (1.0 + gate_act * (1.0 - sigmoid_g))
    ).astype(BF16)
    grad_uact = (grad_hidden * silu_gate).astype(BF16)
    grad_inputs = (
        mm("sh,dh->sd", grad_gact, gate_full) + mm("sh,dh->sd", grad_uact, up_full)
    ).astype(BF16)
    grad_back = exchange(
        grad_inputs.reshape(EXPERTS, SLOTS, MODEL_WIDTH), local_experts, inner
    ).reshape(EXPERTS * SLOTS, MODEL_WIDTH)
    grad_down = grad_to_owners(mm("sh,sd->hd", hidden, grad_recv), inner, cross)
    grad_gate = grad_to_owners(mm("sd,sh->dh", received, grad_gact), inner, cross)
    grad_up = grad_to_owners(mm("sd,sh->dh", received, grad_uact), inner, cross)

    slot_column = slot_gates.reshape(EXPERTS * SLOTS, 1)
    part_one = slot_column.astype(BF16)
    rest = slot_column - part_one.astype(F32)
    part_two = rest.astype(BF16)
    part_three = (rest - part_two.astype(F32)).astype(BF16)
    combined = (
        mm("st,sd->td", place_rows * part_three, returned)
        + mm("st,sd->td", place_rows * part_two, returned)
    ) + mm("st,sd->td", place_rows * part_one, returned)
    layer_out = (middle + combined).astype(BF16)

    products = mm("sd,td->st", returned, cotangent).reshape(EXPERTS, SLOTS, ROWS)
    grad_gates = jnp.sum(jnp.where(place, products, 0.0), axis=1).T
    grad_logits = gates * (grad_gates - jnp.sum(gates * grad_gates, axis=1, keepdims=True))
    grad_logits = (
        grad_logits.reshape(ROWS, local_experts, groups).swapaxes(1, 2).reshape(ROWS, EXPERTS)
    )
    grad_router = jnp.dot(ffn_in.astype(F32).T, grad_logits, precision=HIGH)
    grad_ffn_in = jnp.dot(grad_logits, r_full.astype(F32).T, precision=HIGH)
    grad_ffn_in = grad_ffn_in + mm("st,sd->td", place_rows, grad_back)
    grad_middle, grad_gain_two = norm_back(grad_ffn_in, gain_two, plain_two, scale_two)
    grad_middle = grad_middle + grad_out
    grad_attn = grad_middle.astype(BF16)
    grad_o = sum_to_owners(mm("te,td->ed", mixed, grad_attn).astype(BF16))
    grad_mix = (
        mm("td,ed->te", grad_attn, o_full)
        .astype(BF16)
        .reshape(MB, DEVICE_TOKENS, KEY_VALUE_HEADS, heads, HEAD_SIZE)
    )
    grad_value = mm("bgrqk,bqgrd->bkgd", probs_low, grad_mix).astype(BF16).reshape(ROWS, KV_COLS)
    grad_probs = mm("bqgrd,bkgd->bgrqk", grad_mix, value)
    row_inner = jnp.sum(probs * grad_probs, axis=-1, keepdims=True)
    grad_scores = (probs * (grad_probs - row_inner)).astype(BF16)
    grad_query = mm("bgrqk,bkgd->bqgrd", grad_scores, key) * SCALE
    grad_query = (
        rotary_apply(grad_query.reshape(ROWS, QUERY_HEADS, HEAD_SIZE), cosine, -sine)
        .astype(BF16)
        .reshape(ROWS, Q_COLS)
    )
    grad_key = mm("bgrqk,bqgrd->bkgd", grad_scores, query) * SCALE
    grad_key = (
        rotary_apply(grad_key.reshape(ROWS, KEY_VALUE_HEADS, HEAD_SIZE), cosine, -sine)
        .astype(BF16)
        .reshape(ROWS, KV_COLS)
    )
    grad_qkv = jnp.concatenate([grad_query, grad_key, grad_value], axis=1)
    grad_qkv_w = mm("td,te->de", attention_input, grad_qkv).astype(BF16)
    grad_attn_in = mm("te,de->td", grad_qkv, qkv_full)
    grad_plain, grad_gain_one = norm_back(grad_attn_in, gain_one, plain_one, scale_one)
    small_grads = jnp.concatenate(
        [
            grad_router,
            grad_gain_one[:, None],
            grad_gain_two[:, None],
            jnp.zeros((MODEL_WIDTH, SMALL_COLS // 2 - EXPERTS - 2), F32),
        ],
        axis=1,
    )
    small_high = small_grads.astype(BF16)
    small_low = (small_grads - small_high.astype(F32)).astype(BF16)
    owned = sum_to_owners(jnp.concatenate([grad_qkv_w, small_high, small_low], axis=1))
    small_owned = (
        owned[:, QKV_COLS : QKV_COLS + SMALL_COLS // 2] + owned[:, QKV_COLS + SMALL_COLS // 2 :]
    )
    grad_qkv_w = owned[:, :QKV_COLS]
    return (
        layer_out,
        grad_plain + grad_middle,
        grad_qkv_w[:, :Q_COLS],
        grad_qkv_w[:, Q_COLS : Q_COLS + KV_COLS],
        grad_qkv_w[:, Q_COLS + KV_COLS :],
        grad_o,
        small_owned[:, :EXPERTS],
        small_owned[:, EXPERTS],
        small_owned[:, EXPERTS + 1],
        grad_gate,
        grad_up,
        grad_down,
    )


def solution(mesh):
    in_specs = (
        P(("fsdp", "expert"), None),
        P(("fsdp", "expert"), None),
        P(("fsdp", "expert"), None),
        P(("fsdp", "expert"), None),
        P(("fsdp", "expert"), None),
        P(("fsdp", "expert"), None),
        P(("fsdp", "expert")),
        P(("fsdp", "expert")),
        P("expert", "fsdp", None),
        P("expert", "fsdp", None),
        P("expert", "fsdp", None),
        P(("fsdp", "expert"), None, None),
        P(("fsdp", "expert"), None),
        P(("fsdp", "expert"), None),
    )
    out_specs = (
        P(("fsdp", "expert"), None),
        P(("fsdp", "expert"), None),
        P(("fsdp", "expert"), None),
        P(("fsdp", "expert"), None),
        P(("fsdp", "expert"), None),
        P(("fsdp", "expert"), None),
        P(("fsdp", "expert"), None),
        P(("fsdp", "expert")),
        P(("fsdp", "expert")),
        P("expert", "fsdp", None),
        P("expert", "fsdp", None),
        P("expert", "fsdp", None),
    )
    return jax.shard_map(
        per_device, mesh=mesh, in_specs=in_specs, out_specs=out_specs, check_vma=False
    )
```
